32 devices in a mesh: grp: 2 (over y), seq: 8 (over z, x), mdl: 2 (over core).
Axes of the slice: x: 2, y: 2, z: 4, core: 2. Of those that a mesh axis runs over, the one named last changes fastest.
Arguments:
- signal: bfloat16 [2048, 2048], P(('grp', 'seq'), 'mdl'), parts along dimension 0, may hold values from -6 to 6
- gate_first: bfloat16 [2048, 2048], P(('grp', 'seq'), 'mdl'), parts along dimension 0, may hold values from -6 to 6
- gate_second: bfloat16 [2048, 2048], P(('grp', 'seq'), 'mdl'), parts along dimension 0, may hold values from -6 to 6
- spectrum_first: bfloat16 [2, 16, 128, 2048], P(None, 'seq', None, 'mdl'), may hold values from -8 to 8
- spectrum_second: bfloat16 [2, 16, 128, 2048], P(None, 'seq', None, 'mdl'), may hold values from -8 to 8
- skip_first: float32 [2048], P('mdl'), may hold values from 0.5 to 1.5
- skip_second: float32 [2048], P('mdl'), may hold values from 0.5 to 1.5
- out_weight: bfloat16 [2048, 2048], P('seq', 'mdl'), may hold values from -0.125 to 0.125
Outputs:
- block_out: bfloat16 [2048, 2048], P(('grp', 'seq'), 'mdl'), parts along dimension 0
The draws below stay inside these ranges and needn't reach their ends.
There are 2 independent parts, one for each index of `grp`. The reference program is written for one: setup_inputs(seed, part) draws one part's arguments, and reference() takes and returns one part's arrays. A program takes and returns all parts, laid end to end along the dimension named above; an argument that names none is the same for every part. Nothing has to cross between parts.
All inputs are finite; a program needn't handle non-finite values.
Results may differ from the reference program's by a relative error of at most 0.0057.
Values may be sent and summed in bfloat16 or wider, within the bound.
A program may use at most 64 MiB of HBM per device.

```python
import jax
import jax.numpy as jnp

D = 2048
S_DEV = 128
LENGTH = 1024
COARSE = 16


def level_of(rng, shape, cuts, smallest, high):
    loudness, own = 1.0, jax.random.fold_in(rng, 6)
    for axis_at, blocks in cuts:
        heights = jnp.exp(jax.random.uniform(jax.random.fold_in(own, axis_at), (blocks,), jnp.float32, smallest / len(cuts), high / len(cuts)))
        loudness = loudness * jnp.repeat(heights, shape[axis_at] // blocks).reshape([-1 if axis == axis_at else 1 for axis in range(len(shape))])
    return loudness


def normal_values(own_key, shape, scale, limit, split=(), dtype=jnp.bfloat16):
    array = jax.random.normal(own_key, shape, jnp.float32) * scale
    if len(split) > 0:
        array = level_of(own_key, shape, split, -0.22, 0.18) * array
    return jnp.clip(array, min=-limit, max=limit).astype(dtype)


def setup_inputs(seed: int = 0, part: int = 0) -> dict:
    streams_of = jax.random.split(jax.random.key(seed), 9)
    part_splits = jax.random.split(jax.random.fold_in(streams_of[8], part), 9)
    return {
        "signal": normal_values(part_splits[0], (LENGTH, D), 1.0, 6.0, ((0, 8), (1, 2))),
        "gate_first": normal_values(part_splits[1], (LENGTH, D), 1.0, 6.0, ((0, 8), (1, 2))),
        "gate_second": normal_values(part_splits[2], (LENGTH, D), 1.0, 6.0, ((0, 8), (1, 2))),
        "spectrum_first": normal_values(streams_of[3], (2, COARSE, S_DEV, D), 1.4, 8.0, ((1, 8), (3, 2))),
        "spectrum_second": normal_values(streams_of[4], (2, COARSE, S_DEV, D), 1.4, 8.0, ((1, 8), (3, 2))),
        "skip_first": jnp.clip(0.5 + 1.0 * jax.random.uniform(streams_of[5], (D,), jnp.float32) ** level_of(streams_of[5], (D,), ((0, 2),), -0.2, 0.2), 0.5, 1.5),
        "skip_second": jnp.clip(0.5 + 1.0 * jax.random.uniform(streams_of[6], (D,), jnp.float32) ** level_of(streams_of[6], (D,), ((0, 2),), -0.2, 0.2), 0.5, 1.5),
        "out_weight": normal_values(streams_of[7], (D, D), D ** -0.5, 0.125, ((0, 8), (1, 2))),
    }


def long_filter(field, spectrum):
    total = field.shape[0]
    coarse = spectrum.shape[1]
    fine = spectrum.shape[2]
    width = field.shape[1]
    spec_re = spectrum[0].astype(jnp.float32).transpose(1, 0, 2).reshape(coarse * fine, width)
    spec_im = spectrum[1].astype(jnp.float32).transpose(1, 0, 2).reshape(coarse * fine, width)
    block = 256 if width % 256 == 0 else width
    pieces = []
    for start in range(0, width, block):
        part = field[:, start:start + block]
        padded = jnp.concatenate([part, jnp.zeros_like(part)], axis=0)
        spectra = jnp.fft.fft(padded, axis=0)
        spectra = spectra * (spec_re[:, start:start + block] + 1j * spec_im[:, start:start + block])
        back = jnp.real(jnp.fft.ifft(spectra, axis=0))[:total]
        pieces.append(back)
    return jnp.concatenate(pieces, axis=1)


def reference(signal, gate_first, gate_second, spectrum_first, spectrum_second, skip_first, skip_second, out_weight):
    values = signal.astype(jnp.float32)
    first_conv = long_filter(values, spectrum_first) + skip_first[None, :] * values
    first_out = (gate_first.astype(jnp.float32) * first_conv).astype(jnp.bfloat16)
    first_vals = first_out.astype(jnp.float32)
    second_conv = long_filter(first_vals, spectrum_second) + skip_second[None, :] * first_vals
    mixed = (gate_second.astype(jnp.float32) * second_conv).astype(jnp.bfloat16)
    return jnp.dot(mixed, out_weight, preferred_element_type=jnp.float32).astype(jnp.bfloat16)
```

```python
import functools
import math

import jax
import jax.numpy as jnp
import numpy as np
from jax import lax
from jax.experimental import pallas as pl
from jax.experimental.pallas import tpu as pltpu
from jax.sharding import PartitionSpec as P

MESH = pl.DeviceIdType.MESH
LANES = 128


def angle_grid(first, second, modulus):
    product = first[:, None] * second[None, :] % modulus
    angles = product.astype(jnp.float32) * (2.0 * math.pi / modulus)
    return (jnp.cos(angles), jnp.sin(angles))


def mixing(form, left, right):
    return jnp.einsum(form, left, right, precision=lax.Precision.HIGHEST)


def complex_mix(form, real_table, imag_table, values_re, values_im):
    first_term = mixing(form, real_table, values_re + values_im)
    second_term = mixing(form, real_table + imag_table, values_im)
    third_term = mixing(form, imag_table - real_table, values_re)
    return (first_term - second_term, first_term + third_term)


def channel_filter(field, spectrum):
    coarse = spectrum.shape[1]
    span = spectrum.shape[2]
    count = coarse // 2
    cols = field.shape[1]
    length = coarse * span
    pencil = field.reshape(count, span, cols)
    coarse_ids = jnp.arange(coarse, dtype=jnp.int32)
    cos_a, sin_a = angle_grid(coarse_ids, jnp.arange(count, dtype=jnp.int32), coarse)
    part_re = mixing("ka,amc->kmc", cos_a, pencil)
    part_im = -mixing("ka,amc->kmc", sin_a, pencil)
    fine_ids = jnp.arange(span, dtype=jnp.int32)
    cos_t, sin_t = angle_grid(coarse_ids, fine_ids, length)
    cos_t = cos_t[:, :, None]
    sin_t = sin_t[:, :, None]
    turned_re = part_re * cos_t + part_im * sin_t
    turned_im = part_im * cos_t - part_re * sin_t
    cos_s, sin_s = angle_grid(fine_ids, fine_ids, span)
    full_re, full_im = complex_mix("qm,kmc->kqc", cos_s, -sin_s, turned_re, turned_im)
    filt_re = spectrum[0].astype(jnp.float32)
    filt_im = spectrum[1].astype(jnp.float32)
    prod_re = filt_re * full_re - filt_im * full_im
    prod_im = filt_re * full_im + filt_im * full_re
    inner_re, inner_im = complex_mix("mq,kqc->kmc", cos_s, sin_s, prod_re, prod_im)
    back_re = inner_re * cos_t - inner_im * sin_t
    back_im = inner_im * cos_t + inner_re * sin_t
    result = mixing("ka,kmc->amc", cos_a, back_re) - mixing("ka,kmc->amc", sin_a, back_im)
    return (result / length).reshape(count * span, cols)


def plain_shards(
    signal,
    gate_first,
    gate_second,
    spectrum_first,
    spectrum_second,
    skip_first,
    skip_second,
    out_weight,
):
    seq_index = lax.axis_index("seq")
    width = signal.shape[1]
    parts_seq = lax.axis_size("seq")
    cols = width // parts_seq
    col_sig, col_first, col_second = (
        lax.all_to_all(signal, "seq", split_axis=1, concat_axis=0, tiled=True),
        lax.all_to_all(gate_first, "seq", split_axis=1, concat_axis=0, tiled=True),
        lax.all_to_all(gate_second, "seq", split_axis=1, concat_axis=0, tiled=True),
    )
    spec_one, spec_two = (
        lax.all_to_all(spectrum_first, "seq", split_axis=3, concat_axis=1, tiled=True),
        lax.all_to_all(spectrum_second, "seq", split_axis=3, concat_axis=1, tiled=True),
    )
    skip_one = lax.dynamic_slice_in_dim(skip_first, seq_index * cols, cols, 0)
    skip_two = lax.dynamic_slice_in_dim(skip_second, seq_index * cols, cols, 0)
    values = col_sig.astype(jnp.float32)
    first_conv = channel_filter(values, spec_one) + skip_one * values
    first_out = (col_first.astype(jnp.float32) * first_conv).astype(jnp.bfloat16)
    first_vals = first_out.astype(jnp.float32)
    second_conv = channel_filter(first_vals, spec_two) + skip_two * first_vals
    mixed_cols = (col_second.astype(jnp.float32) * second_conv).astype(jnp.bfloat16)
    mixed = lax.all_to_all(mixed_cols, "seq", split_axis=0, concat_axis=1, tiled=True)
    features = lax.all_gather(mixed, "mdl", axis=1, tiled=True)
    total = jnp.dot(
        features,
        lax.all_gather(out_weight, "seq", axis=0, tiled=True),
        preferred_element_type=jnp.float32,
    )
    return total.astype(jnp.bfloat16)


def turn_tables(span, coarse):
    ids = np.arange(span)
    fine = 2.0 * math.pi * (ids[:, None] * ids[None, :] % span) / span
    step = 2.0 * math.pi * np.broadcast_to(ids[:, None], (span, span)) / (span * coarse)
    return np.stack(
        [np.cos(fine), np.sin(fine), np.cos(step), np.sin(step), np.cos(step).T, np.sin(step).T]
    ).astype(np.float32)


def weighted(terms):
    total = None
    for weight, value in terms:
        if abs(weight) < 1e-12:
            continue
        if abs(weight - 1.0) < 1e-12:
            term = value
        elif abs(weight + 1.0) < 1e-12:
            total = -value if total is None else total - value
            continue
        else:
            term = value * weight
        total = term if total is None else total + term
    return total


def coarse_forward(field, parts, rows):
    count, span, cols = field.shape
    half = count // 2

    @pl.loop(0, span // rows)
    def _(i):
        at = pl.multiple_of(i * rows, rows)
        f = [field[a, pl.ds(at, rows), :].astype(jnp.float32) for a in range(count)]
        plus = {a: f[a] + f[count - a] for a in range(1, half)}
        minus = {a: f[a] - f[count - a] for a in range(1, half)}
        for j in range(count + 1):
            for_cos, for_sin = (plus, minus) if j % 2 == 0 else (minus, plus)
            angle = [math.pi * a * j / count for a in range(count)]
            real = weighted(
                [(1.0, f[0]), (math.cos(angle[half]), f[half])]
                + [(math.cos(angle[a]), for_cos[a]) for a in range(1, half)]
            )
            imag = weighted(
                [(-math.sin(angle[half]), f[half])]
                + [(-math.sin(angle[a]), for_sin[a]) for a in range(1, half)]
            )
            if imag is None:
                imag = jnp.zeros_like(real)
            parts[j, pl.ds(at, rows), :] = real.astype(jnp.bfloat16)
            parts[j, pl.ds(pl.multiple_of(span + at, rows), rows), :] = imag.astype(jnp.bfloat16)


def fine_stage(parts, spectrum, there, back_table, back, k, count, span):
    @pl.loop(0, count)
    def _(b):
        j = 2 * b + k
        source = jnp.where(j <= count, j, 2 * count - j)
        full = jnp.dot(there[j], parts[source], preferred_element_type=jnp.float32)
        full_re, full_im = full[:span], full[span:]
        filt_re = spectrum[k, b, 0].astype(jnp.float32)
        filt_im = spectrum[k, b, 1].astype(jnp.float32)
        prod_re = filt_re * full_re - filt_im * full_im
        prod_im = filt_re * full_im + filt_im * full_re
        prod = jnp.concatenate([prod_re.astype(jnp.bfloat16), prod_im.astype(jnp.bfloat16)], axis=0)
        back[j] = jnp.dot(back_table[j], prod, preferred_element_type=jnp.float32)


def coarse_back(back, field, gate, skip, result, rows):
    count, span, cols = field.shape
    half = count // 2
    direct = jnp.broadcast_to(skip, (rows, cols))

    @pl.loop(0, span // rows)
    def _(i):
        at = pl.multiple_of(i * rows, rows)
        low = pl.multiple_of(span + at, rows)

        def real(j):
            return back[j, pl.ds(at, rows), :]

        def imag(j):
            return back[j, pl.ds(low, rows), :]

        re = [real(0)] + [real(j) + real(2 * count - j) for j in range(1, count)] + [real(count)]
        im = [None] + [imag(j) - imag(2 * count - j) for j in range(1, count)] + [None]
        even_re = [re[j] + re[count - j] for j in range(half)]
        odd_re = [re[j] - re[count - j] for j in range(half)]
        even_im = [None] + [im[j] - im[count - j] for j in range(1, half)]
        odd_im = [None] + [im[j] + im[count - j] for j in range(1, half)]
        for a in range(count):
            use_re, use_im = (even_re, even_im) if a % 2 == 0 else (odd_re, odd_im)
            angle = [math.pi * a * j / count for j in range(half + 1)]
            total = weighted(
                [(math.cos(angle[j]), use_re[j]) for j in range(half)]
                + [(math.cos(angle[half]), re[half]), (-math.sin(angle[half]), im[half])]
                + [(-math.sin(angle[j]), use_im[j]) for j in range(1, half)]
            )
            values = field[a, pl.ds(at, rows), :].astype(jnp.float32)
            total = total + direct * values
            gated = gate[a, pl.ds(at, rows), :].astype(jnp.float32) * total
            result[a, pl.ds(at, rows), :] = gated.astype(jnp.bfloat16)


def build_tables(tab, there, back_table, turn, count, span):
    turn[0] = tab[0]
    turn[1] = tab[1]
    turn[2] = tab[0]
    turn[3] = tab[1]
    scale = 1.0 / (2 * count * span)

    @pl.loop(0, 2 * count)
    def _(j):
        flip = jnp.where(j > count, -1.0, 1.0).astype(jnp.float32)
        cos_a, sin_a, cos_b, sin_b = turn[0], turn[1], turn[2], turn[3]
        there[j, :span, :span] = cos_a.astype(jnp.bfloat16)
        there[j, :span, span:] = (sin_a * flip).astype(jnp.bfloat16)
        there[j, span:, :span] = (-sin_a).astype(jnp.bfloat16)
        there[j, span:, span:] = (cos_a * flip).astype(jnp.bfloat16)
        cos_s, sin_s = cos_b * scale, sin_b * scale
        back_table[j, :span, :span] = cos_s.astype(jnp.bfloat16)
        back_table[j, :span, span:] = (-sin_s).astype(jnp.bfloat16)
        back_table[j, span:, :span] = sin_s.astype(jnp.bfloat16)
        back_table[j, span:, span:] = cos_s.astype(jnp.bfloat16)
        turn[0] = cos_a * tab[4] - sin_a * tab[5]
        turn[1] = sin_a * tab[4] + cos_a * tab[5]
        turn[2] = cos_b * tab[2] - sin_b * tab[3]
        turn[3] = sin_b * tab[2] + cos_b * tab[3]


def block_kernel(
    count,
    signal,
    gate_one,
    gate_two,
    spec_one,
    spec_two,
    skip_one,
    skip_two,
    tab,
    out,
    in_signal,
    in_gate_one,
    in_gate_two,
    in_spec_one,
    in_spec_two,
    in_skip,
    there,
    back_table,
    turn,
    parts,
    back,
    second_field,
    mixed,
    send_sem,
    own_sem,
    recv_sem,
):
    g, s, m = lax.axis_index("grp"), lax.axis_index("seq"), lax.axis_index("mdl")
    span, cols = in_signal.shape[1], in_signal.shape[2]
    total = 4 * count
    me = (g * count + s) * 2 + m

    barrier = pltpu.get_barrier_semaphore()

    @pl.loop(1, total)
    def _(o):
        peer = lax.rem(me + o, total)
        pl.semaphore_signal(
            barrier,
            inc=1,
            device_id=(peer // (2 * count), lax.rem(peer // 2, count), lax.rem(peer, 2)),
            device_id_type=MESH,
        )

    pl.semaphore_wait(barrier, total - 1)

    def columns(block):
        return pl.ds(pl.multiple_of(block * cols, cols), cols)

    def remote(source, target, slot, own, where):
        return pltpu.make_async_remote_copy(
            src_ref=source,
            dst_ref=target,
            send_sem=own_sem.at[slot] if own else send_sem.at[slot],
            recv_sem=recv_sem.at[slot],
            device_id=where,
            device_id_type=MESH,
        )

    def local(source, target, slot):
        return pltpu.make_async_copy(source, target, recv_sem.at[slot])

    def swap(source, target, slot):
        @pl.when(g == m)
        def _():
            local(source, target, slot).start()

        @pl.when(g != m)
        def _():
            remote(source, target, slot, True, (m, s, g)).start()

    def send_rows(array, buffer, slot):
        @pl.loop(1, count)
        def _(o):
            c = lax.rem(s + o, count)
            remote(array.at[:, columns(c)], buffer.at[s], slot, False, (m, c, g)).start()

        swap(array.at[:, columns(s)], buffer.at[s], slot)

    def send_spectrum(array, buffer, slot):
        @pl.when(g == m)
        def _():
            @pl.loop(1, count)
            def _(o):
                c = lax.rem(s + o, count)
                for k in range(2):
                    remote(
                        array.at[:, k, :, columns(c)], buffer.at[k, s], slot, False, (g, c, k)
                    ).start()

            remote(
                array.at[:, 1 - m, :, columns(s)], buffer.at[1 - m, s], slot, True, (g, s, 1 - m)
            ).start()
            local(array.at[:, m, :, columns(s)], buffer.at[m, s], slot).start()

    def relay(buffer, slot):
        return remote(buffer.at[m], buffer.at[m], slot, False, (g, s, 1 - m))

    def take(view, slot):
        pltpu.make_async_copy(view, view, recv_sem.at[slot]).wait()

    send_rows(signal, in_signal, 0)
    send_spectrum(spec_one, in_spec_one, 3)
    send_rows(gate_one, in_gate_one, 1)
    swap(skip_one, in_skip.at[0], 7)
    swap(skip_two, in_skip.at[1], 8)
    send_spectrum(spec_two, in_spec_two, 5)
    send_rows(gate_two, in_gate_two, 2)

    build_tables(tab, there, back_table, turn, count, span)

    take(in_signal, 0)
    coarse_forward(in_signal, parts, 16)
    take(in_spec_one.at[m], 3)
    relay(in_spec_one, 4).start()
    fine_stage(parts, in_spec_one, there, back_table, back, m, count, span)
    take(in_spec_one.at[1 - m], 4)
    fine_stage(parts, in_spec_one, there, back_table, back, 1 - m, count, span)
    take(in_gate_one, 1)
    take(in_skip.at[0], 7)
    take(in_skip.at[1], 8)
    coarse_back(back, in_signal, in_gate_one, in_skip[0, pl.ds(s, 1), :], second_field, 16)
    coarse_forward(second_field, parts, 16)
    take(in_spec_two.at[m], 5)
    relay(in_spec_two, 6).start()
    fine_stage(parts, in_spec_two, there, back_table, back, m, count, span)
    take(in_spec_two.at[1 - m], 6)
    fine_stage(parts, in_spec_two, there, back_table, back, 1 - m, count, span)
    take(in_gate_two, 2)
    coarse_back(back, second_field, in_gate_two, in_skip[1, pl.ds(s, 1), :], mixed, 16)

    width = count * cols
    mine = columns(g * count + s)

    @pl.loop(1, count)
    def _(o):
        c = lax.rem(s + o, count)
        remote(mixed.at[c], out.at[:, mine], 9, False, (m, c, g)).start()

    swap(mixed.at[s], out.at[:, mine], 9)
    half = out.at[:, pl.ds(pl.multiple_of(m * width, width), width)]
    other = out.at[:, pl.ds(pl.multiple_of((1 - m) * width, width), width)]
    take(half, 9)
    final = remote(half, half, 10, False, (g, s, 1 - m))
    final.start()
    take(other, 10)

    def sent(view, slot, own=False):
        pltpu.make_async_copy(view, view, own_sem.at[slot] if own else send_sem.at[slot]).wait()

    final.wait_send()
    relay(in_spec_one, 4).wait_send()
    relay(in_spec_two, 6).wait_send()
    most = pl.ds(0, count - 1)
    for slot in (0, 1, 2, 9):
        sent(in_signal.at[most], slot)

    @pl.when(g != m)
    def _():
        for slot in (0, 1, 2, 9):
            sent(in_signal.at[0], slot, True)
        sent(in_skip.at[0], 7, True)
        sent(in_skip.at[1], 8, True)

    @pl.when(g == m)
    def _():
        for slot in (3, 5):
            sent(in_spec_one.at[:, most], slot)
            sent(in_spec_one.at[0, 0], slot, True)


def direct_shards(
    signal,
    gate_first,
    gate_second,
    spectrum_first,
    spectrum_second,
    skip_first,
    skip_second,
    out_weight,
):
    count = lax.axis_size("seq")
    span, width = signal.shape
    cols = width // count
    coarse = 2 * count
    weight = lax.all_gather(out_weight, "seq", axis=0, tiled=True)
    anywhere = pl.BlockSpec(memory_space=pl.ANY)
    vmem = pl.BlockSpec(memory_space=pltpu.VMEM)
    bf16, f32 = jnp.bfloat16, jnp.float32
    features = pl.pallas_call(
        functools.partial(block_kernel, count),
        out_shape=jax.ShapeDtypeStruct((span, 2 * width), bf16),
        in_specs=[anywhere] * 7 + [vmem],
        out_specs=vmem,
        scratch_shapes=[
            pltpu.VMEM((count, span, cols), bf16),
            pltpu.VMEM((count, span, cols), bf16),
            pltpu.VMEM((count, span, cols), bf16),
            pltpu.VMEM((2, count, 2, span, cols), bf16),
            pltpu.VMEM((2, count, 2, span, cols), bf16),
            pltpu.VMEM((2, count, cols), f32),
            pltpu.VMEM((coarse, 2 * span, 2 * span), bf16),
            pltpu.VMEM((coarse, 2 * span, 2 * span), bf16),
            pltpu.VMEM((4, span, span), f32),
            pltpu.VMEM((count + 1, 2 * span, cols), bf16),
            pltpu.VMEM((coarse, 2 * span, cols), f32),
            pltpu.VMEM((count, span, cols), bf16),
            pltpu.VMEM((count, span, cols), bf16),
            pltpu.SemaphoreType.DMA((11,)),
            pltpu.SemaphoreType.DMA((11,)),
            pltpu.SemaphoreType.DMA((11,)),
        ],
        compiler_params=pltpu.CompilerParams(
            collective_id=0, has_side_effects=True, vmem_limit_bytes=32 * 1024 * 1024
        ),
        cost_estimate=pl.CostEstimate(
            flops=16 * coarse * span * span * cols, bytes_accessed=1 << 26, transcendentals=0
        ),
    )(
        signal,
        gate_first,
        gate_second,
        spectrum_first,
        spectrum_second,
        skip_first.reshape(count, cols),
        skip_second.reshape(count, cols),
        jnp.asarray(turn_tables(span, coarse)),
    )
    total = jnp.dot(features, weight, preferred_element_type=jnp.float32)
    return total.astype(jnp.bfloat16)


def shards(*arrays):
    count = lax.axis_size("seq")
    span, width = arrays[0].shape
    pairs = lax.axis_size("grp") == 2 and lax.axis_size("mdl") == 2
    whole_tiles = width == count * LANES and span == LANES and count % 8 == 0 and count <= 16
    if pairs and whole_tiles and arrays[3].shape[1] == 2:
        return direct_shards(*arrays)
    return plain_shards(*arrays)


def solution(mesh):
    placed = (
        P(("grp", "seq"), "mdl"),
        P(("grp", "seq"), "mdl"),
        P(("grp", "seq"), "mdl"),
        P(None, "seq", None, "mdl"),
        P(None, "seq", None, "mdl"),
        P("mdl"),
        P("mdl"),
        P("seq", "mdl"),
    )
    return jax.shard_map(
        shards, mesh=mesh, in_specs=placed, out_specs=P(("grp", "seq"), "mdl"), check_vma=False
    )
```

```python
import functools
import math

import jax
import jax.numpy as jnp
import numpy as np
from jax import lax
from jax.experimental import pallas as pl
from jax.experimental.pallas import tpu as pltpu
from jax.sharding import PartitionSpec as P

MESH = pl.DeviceIdType.MESH
LANES = 128


def angle_grid(first, second, modulus):
    product = first[:, None] * second[None, :] % modulus
    angles = product.astype(jnp.float32) * (2.0 * math.pi / modulus)
    return (jnp.cos(angles), jnp.sin(angles))


def mixing(form, left, right):
    return jnp.einsum(form, left, right, precision=lax.Precision.HIGHEST)


def complex_mix(form, real_table, imag_table, values_re, values_im):
    first_term = mixing(form, real_table, values_re + values_im)
    second_term = mixing(form, real_table + imag_table, values_im)
    third_term = mixing(form, imag_table - real_table, values_re)
    return (first_term - second_term, first_term + third_term)


def channel_filter(field, spectrum):
    coarse = spectrum.shape[1]
    span = spectrum.shape[2]
    count = coarse // 2
    cols = field.shape[1]
    length = coarse * span
    pencil = field.reshape(count, span, cols)
    coarse_ids = jnp.arange(coarse, dtype=jnp.int32)
    cos_a, sin_a = angle_grid(coarse_ids, jnp.arange(count, dtype=jnp.int32), coarse)
    part_re = mixing("ka,amc->kmc", cos_a, pencil)
    part_im = -mixing("ka,amc->kmc", sin_a, pencil)
    fine_ids = jnp.arange(span, dtype=jnp.int32)
    cos_t, sin_t = angle_grid(coarse_ids, fine_ids, length)
    cos_t = cos_t[:, :, None]
    sin_t = sin_t[:, :, None]
    turned_re = part_re * cos_t + part_im * sin_t
    turned_im = part_im * cos_t - part_re * sin_t
    cos_s, sin_s = angle_grid(fine_ids, fine_ids, span)
    full_re, full_im = complex_mix("qm,kmc->kqc", cos_s, -sin_s, turned_re, turned_im)
    filt_re = spectrum[0].astype(jnp.float32)
    filt_im = spectrum[1].astype(jnp.float32)
    prod_re = filt_re * full_re - filt_im * full_im
    prod_im = filt_re * full_im + filt_im * full_re
    inner_re, inner_im = complex_mix("mq,kqc->kmc", cos_s, sin_s, prod_re, prod_im)
    back_re = inner_re * cos_t - inner_im * sin_t
    back_im = inner_im * cos_t + inner_re * sin_t
    result = mixing("ka,kmc->amc", cos_a, back_re) - mixing("ka,kmc->amc", sin_a, back_im)
    return (result / length).reshape(count * span, cols)


def plain_shards(
    signal,
    gate_first,
    gate_second,
    spectrum_first,
    spectrum_second,
    skip_first,
    skip_second,
    out_weight,
):
    seq_index = lax.axis_index("seq")
    width = signal.shape[1]
    parts_seq = lax.axis_size("seq")
    cols = width // parts_seq
    col_sig, col_first, col_second = (
        lax.all_to_all(signal, "seq", split_axis=1, concat_axis=0, tiled=True),
        lax.all_to_all(gate_first, "seq", split_axis=1, concat_axis=0, tiled=True),
        lax.all_to_all(gate_second, "seq", split_axis=1, concat_axis=0, tiled=True),
    )
    spec_one, spec_two = (
        lax.all_to_all(spectrum_first, "seq", split_axis=3, concat_axis=1, tiled=True),
        lax.all_to_all(spectrum_second, "seq", split_axis=3, concat_axis=1, tiled=True),
    )
    skip_one = lax.dynamic_slice_in_dim(skip_first, seq_index * cols, cols, 0)
    skip_two = lax.dynamic_slice_in_dim(skip_second, seq_index * cols, cols, 0)
    values = col_sig.astype(jnp.float32)
    first_conv = channel_filter(values, spec_one) + skip_one * values
    first_out = (col_first.astype(jnp.float32) * first_conv).astype(jnp.bfloat16)
    first_vals = first_out.astype(jnp.float32)
    second_conv = channel_filter(first_vals, spec_two) + skip_two * first_vals
    mixed_cols = (col_second.astype(jnp.float32) * second_conv).astype(jnp.bfloat16)
    mixed = lax.all_to_all(mixed_cols, "seq", split_axis=0, concat_axis=1, tiled=True)
    features = lax.all_gather(mixed, "mdl", axis=1, tiled=True)
    total = jnp.dot(
        features,
        lax.all_gather(out_weight, "seq", axis=0, tiled=True),
        preferred_element_type=jnp.float32,
    )
    return total.astype(jnp.bfloat16)


def turn_tables(span, coarse):
    ids = np.arange(span)
    fine = 2.0 * math.pi * (ids[:, None] * ids[None, :] % span) / span
    step = 2.0 * math.pi * np.broadcast_to(ids[:, None], (span, span)) / (span * coarse)
    return np.stack(
        [np.cos(fine), np.sin(fine), np.cos(step), np.sin(step), np.cos(step).T, np.sin(step).T]
    ).astype(np.float32)


def weighted(terms):
    total = None
    for weight, value in terms:
        if abs(weight) < 1e-12:
            continue
        if abs(weight - 1.0) < 1e-12:
            term = value
        elif abs(weight + 1.0) < 1e-12:
            total = -value if total is None else total - value
            continue
        else:
            term = value * weight
        total = term if total is None else total + term
    return total


def coarse_forward(field, parts, rows):
    count, span, cols = field.shape
    half = count // 2

    @pl.loop(0, span // rows)
    def _(i):
        at = pl.multiple_of(i * rows, rows)
        f = [field[a, pl.ds(at, rows), :].astype(jnp.float32) for a in range(count)]
        plus = {a: f[a] + f[count - a] for a in range(1, half)}
        minus = {a: f[a] - f[count - a] for a in range(1, half)}
        for j in range(count + 1):
            for_cos, for_sin = (plus, minus) if j % 2 == 0 else (minus, plus)
            angle = [math.pi * a * j / count for a in range(count)]
            real = weighted(
                [(1.0, f[0]), (math.cos(angle[half]), f[half])]
                + [(math.cos(angle[a]), for_cos[a]) for a in range(1, half)]
            )
            imag = weighted(
                [(-math.sin(angle[half]), f[half])]
                + [(-math.sin(angle[a]), for_sin[a]) for a in range(1, half)]
            )
            if imag is None:
                imag = jnp.zeros_like(real)
            for top, value in ((at, real), (pl.multiple_of(span + at, rows), imag)):
                high = value.astype(jnp.bfloat16)
                parts[j, pl.ds(top, rows), :cols] = high
                parts[j, pl.ds(top, rows), cols:] = (value - high.astype(jnp.float32)).astype(
                    jnp.bfloat16
                )


def split_dot(table, j, both, cols):
    main = jnp.dot(table[j, 0], both, preferred_element_type=jnp.float32)
    rest = jnp.dot(table[j, 1], both[:, :cols], preferred_element_type=jnp.float32)
    return main[:, :cols] + (main[:, cols:] + rest)


def fine_stage(parts, spectrum, there, back_table, back, k, count, span):
    @pl.loop(0, count)
    def _(b):
        j = 2 * b + k
        source = jnp.where(j <= count, j, 2 * count - j)
        full = split_dot(there, j, parts[source], back.shape[2])
        full_re, full_im = full[:span], full[span:]
        filt_re = spectrum[k, b, 0].astype(jnp.float32)
        filt_im = spectrum[k, b, 1].astype(jnp.float32)
        prod_re = filt_re * full_re - filt_im * full_im
        prod_im = filt_re * full_im + filt_im * full_re
        prod = jnp.concatenate([prod_re, prod_im], axis=0)
        high = prod.astype(jnp.bfloat16)
        low = (prod - high.astype(jnp.float32)).astype(jnp.bfloat16)
        both = jnp.concatenate([high, low], axis=1)
        back[j] = split_dot(back_table, j, both, back.shape[2])


def coarse_back(back, field, gate, skip, result, rows):
    count, span, cols = field.shape
    half = count // 2
    direct = jnp.broadcast_to(skip, (rows, cols))

    @pl.loop(0, span // rows)
    def _(i):
        at = pl.multiple_of(i * rows, rows)
        low = pl.multiple_of(span + at, rows)

        def real(j):
            return back[j, pl.ds(at, rows), :]

        def imag(j):
            return back[j, pl.ds(low, rows), :]

        re = [real(0)] + [real(j) + real(2 * count - j) for j in range(1, count)] + [real(count)]
        im = [None] + [imag(j) - imag(2 * count - j) for j in range(1, count)] + [None]
        even_re = [re[j] + re[count - j] for j in range(half)]
        odd_re = [re[j] - re[count - j] for j in range(half)]
        even_im = [None] + [im[j] - im[count - j] for j in range(1, half)]
        odd_im = [None] + [im[j] + im[count - j] for j in range(1, half)]
        for a in range(count):
            use_re, use_im = (even_re, even_im) if a % 2 == 0 else (odd_re, odd_im)
            angle = [math.pi * a * j / count for j in range(half + 1)]
            total = weighted(
                [(math.cos(angle[j]), use_re[j]) for j in range(half)]
                + [(math.cos(angle[half]), re[half]), (-math.sin(angle[half]), im[half])]
                + [(-math.sin(angle[j]), use_im[j]) for j in range(1, half)]
            )
            values = field[a, pl.ds(at, rows), :].astype(jnp.float32)
            total = total + direct * values
            gated = gate[a, pl.ds(at, rows), :].astype(jnp.float32) * total
            result[a, pl.ds(at, rows), :] = gated.astype(jnp.bfloat16)


def build_tables(tab, there, back_table, turn, count, span):
    turn[0] = tab[0]
    turn[1] = tab[1]
    turn[2] = tab[0]
    turn[3] = tab[1]
    scale = 1.0 / (2 * count * span)

    @pl.loop(0, 2 * count)
    def _(j):
        flip = jnp.where(j > count, -1.0, 1.0).astype(jnp.float32)
        cos_a, sin_a, cos_b, sin_b = turn[0], turn[1], turn[2], turn[3]
        cos_s, sin_s = cos_b * scale, sin_b * scale
        entries = (
            (there, cos_a, sin_a * flip, -sin_a, cos_a * flip),
            (back_table, cos_s, -sin_s, sin_s, cos_s),
        )
        places = ((0, 0), (0, 1), (1, 0), (1, 1))
        for table, *blocks in entries:
            for (row, col), value in zip(places, blocks):
                at = (slice(row * span, row * span + span), slice(col * span, col * span + span))
                high = value.astype(jnp.bfloat16)
                table[(j, 0) + at] = high
                table[(j, 1) + at] = (value - high.astype(jnp.float32)).astype(jnp.bfloat16)
        turn[0] = cos_a * tab[4] - sin_a * tab[5]
        turn[1] = sin_a * tab[4] + cos_a * tab[5]
        turn[2] = cos_b * tab[2] - sin_b * tab[3]
        turn[3] = sin_b * tab[2] + cos_b * tab[3]


def block_kernel(
    count,
    signal,
    gate_one,
    gate_two,
    spec_one,
    spec_two,
    skip_one,
    skip_two,
    weight,
    tab,
    out,
    in_signal,
    in_gate_one,
    in_gate_two,
    in_spec_one,
    in_spec_two,
    in_skip,
    there,
    back_table,
    turn,
    parts,
    back,
    second_field,
    mixed,
    features,
    totals,
    rows_all,
    send_sem,
    own_sem,
    recv_sem,
    line_send,
    line_recv,
    side_send,
    side_recv,
    plane_send,
    plane_recv,
    own_copy,
):
    g, s, m = lax.axis_index("grp"), lax.axis_index("seq"), lax.axis_index("mdl")
    span, cols = in_signal.shape[1], in_signal.shape[2]
    total = 4 * count
    me = (g * count + s) * 2 + m

    barrier = pltpu.get_barrier_semaphore()

    @pl.loop(1, total)
    def _(o):
        peer = lax.rem(me + o, total)
        pl.semaphore_signal(
            barrier,
            inc=1,
            device_id=(peer // (2 * count), lax.rem(peer // 2, count), lax.rem(peer, 2)),
            device_id_type=MESH,
        )

    pl.semaphore_wait(barrier, total - 1)

    def columns(block):
        return pl.ds(pl.multiple_of(block * cols, cols), cols)

    def remote(source, target, slot, own, where):
        return pltpu.make_async_remote_copy(
            src_ref=source,
            dst_ref=target,
            send_sem=own_sem.at[slot] if own else send_sem.at[slot],
            recv_sem=recv_sem.at[slot],
            device_id=where,
            device_id_type=MESH,
        )

    def local(source, target, slot):
        return pltpu.make_async_copy(source, target, recv_sem.at[slot])

    def swap(source, target, slot):
        @pl.when(g == m)
        def _():
            local(source, target, slot).start()

        @pl.when(g != m)
        def _():
            remote(source, target, slot, True, (m, s, g)).start()

    def send_rows(array, buffer, slot):
        @pl.loop(1, count)
        def _(o):
            c = lax.rem(s + o, count)
            remote(array.at[:, columns(c)], buffer.at[s], slot, False, (m, c, g)).start()

        swap(array.at[:, columns(s)], buffer.at[s], slot)

    def send_spectrum(array, buffer, slot):
        @pl.when(g == m)
        def _():
            @pl.loop(1, count)
            def _(o):
                c = lax.rem(s + o, count)
                for k in range(2):
                    remote(
                        array.at[:, k, :, columns(c)], buffer.at[k, s], slot, False, (g, c, k)
                    ).start()

            remote(
                array.at[:, 1 - m, :, columns(s)], buffer.at[1 - m, s], slot, True, (g, s, 1 - m)
            ).start()
            local(array.at[:, m, :, columns(s)], buffer.at[m, s], slot).start()

    def relay(buffer, slot):
        return remote(buffer.at[m], buffer.at[m], slot, False, (g, s, 1 - m))

    def take(view, slot):
        pltpu.make_async_copy(view, view, recv_sem.at[slot]).wait()

    levels = count // 2
    z, x = s // 2, lax.rem(s, 2)
    beside = s + 1 - 2 * x
    depth = weight.shape[0]
    piece = depth // 2

    def chunk(block, half):
        return rows_all.at[pl.ds(pl.multiple_of(block * depth + half * piece, piece), piece), :]

    def post(block, source, sems, where):
        return pltpu.make_async_remote_copy(
            src_ref=source,
            dst_ref=chunk(block, g),
            send_sem=sems[0],
            recv_sem=sems[1],
            device_id=where,
            device_id_type=MESH,
        )

    def along(block, source, way):
        level = block // 2
        step = 2 if way == 0 else -2
        return post(
            block, source, (line_send.at[way, level], line_recv.at[level]), (g, s + step, m)
        )

    def across(block, source):
        level = block // 2
        return post(block, source, (side_send.at[level], side_recv.at[level]), (g, beside, m))

    def over(block):
        return post(
            block, chunk(block, g), (plane_send.at[block], plane_recv.at[block]), (1 - g, s, m)
        )

    def landed(block, half, sem):
        view = chunk(block, half)
        pltpu.make_async_copy(view, view, sem).wait()

    own_rows = pltpu.make_async_copy(
        weight, rows_all.at[pl.ds(pl.multiple_of(s * depth, depth), depth), :], own_copy.at[0]
    )
    own_piece = weight.at[pl.ds(pl.multiple_of(g * piece, piece), piece), :]

    def weight_step(distance):
        if distance == 0:
            own_rows.start()

            @pl.when(z < levels - 1)
            def _():
                along(s, own_piece, 0).start()

            @pl.when(z > 0)
            def _():
                along(s, own_piece, 1).start()

            across(s, own_piece).start()
            return

        @pl.when(z >= distance)
        def _():
            block = s - 2 * distance
            landed(block, g, line_recv.at[z - distance])

            @pl.when(z < levels - 1)
            def _():
                along(block, chunk(block, g), 0).start()

            across(block, chunk(block, g)).start()
            over(block).start()

        @pl.when(z + distance < levels)
        def _():
            block = s + 2 * distance
            landed(block, g, line_recv.at[z + distance])

            @pl.when(z > 0)
            def _():
                along(block, chunk(block, g), 1).start()

            across(block, chunk(block, g)).start()
            over(block).start()

    def weight_side(distance):
        @pl.when(z >= distance)
        def _():
            block = beside - 2 * distance
            landed(block, g, side_recv.at[z - distance])
            over(block).start()

        if distance > 0:

            @pl.when(z + distance < levels)
            def _():
                block = beside + 2 * distance
                landed(block, g, side_recv.at[z + distance])
                over(block).start()

    def weight_end():
        own_rows.wait()

        @pl.loop(1, count)
        def _(o):
            block = lax.rem(s + o, count)
            landed(block, 1 - g, plane_recv.at[block])

    def weight_sent():
        for distance in range(levels):

            @pl.when((z >= distance) & (z < levels - 1))
            def _():
                along(s - 2 * distance, chunk(0, g), 0).wait_send()

            @pl.when((z + distance < levels) & (z > 0))
            def _():
                along(s + 2 * distance, chunk(0, g), 1).wait_send()

        @pl.loop(0, levels)
        def _(level):
            across(2 * level + x, chunk(0, g)).wait_send()

        @pl.loop(1, count)
        def _(o):
            over(lax.rem(s + o, count)).wait_send()

    send_rows(signal, in_signal, 0)
    weight_step(0)
    send_spectrum(spec_one, in_spec_one, 3)
    send_rows(gate_one, in_gate_one, 1)
    swap(skip_one, in_skip.at[0], 7)
    swap(skip_two, in_skip.at[1], 8)

    build_tables(tab, there, back_table, turn, count, span)

    weight_step(1)
    weight_side(0)
    send_spectrum(spec_two, in_spec_two, 5)
    send_rows(gate_two, in_gate_two, 2)
    take(in_signal, 0)
    coarse_forward(in_signal, parts, 16)
    weight_step(2)
    weight_side(1)
    take(in_spec_one.at[m], 3)
    relay(in_spec_one, 4).start()
    fine_stage(parts, in_spec_one, there, back_table, back, m, count, span)
    weight_step(3)
    weight_side(2)
    take(in_spec_one.at[1 - m], 4)
    fine_stage(parts, in_spec_one, there, back_table, back, 1 - m, count, span)
    take(in_gate_one, 1)
    take(in_skip.at[0], 7)
    take(in_skip.at[1], 8)
    coarse_back(back, in_signal, in_gate_one, in_skip[0, pl.ds(s, 1), :], second_field, 16)
    weight_side(3)
    coarse_forward(second_field, parts, 16)
    take(in_spec_two.at[m], 5)
    relay(in_spec_two, 6).start()
    fine_stage(parts, in_spec_two, there, back_table, back, m, count, span)
    take(in_spec_two.at[1 - m], 6)
    fine_stage(parts, in_spec_two, there, back_table, back, 1 - m, count, span)
    take(in_gate_two, 2)
    coarse_back(back, second_field, in_gate_two, in_skip[1, pl.ds(s, 1), :], mixed, 16)

    width = count * cols
    mine = columns(g * count + s)

    @pl.loop(1, count)
    def _(o):
        c = lax.rem(s + o, count)
        remote(mixed.at[c], features.at[:, mine], 9, False, (m, c, g)).start()

    swap(mixed.at[s], features.at[:, mine], 9)
    weight_end()
    first = pl.multiple_of(m * width, width)
    second = pl.multiple_of((1 - m) * width, width)
    half = features.at[:, pl.ds(first, width)]
    other = features.at[:, pl.ds(second, width)]
    take(half, 9)
    final = remote(half, half, 10, False, (g, s, 1 - m))
    final.start()
    tile = 2 * cols

    @pl.loop(0, width // tile)
    def _(i):
        at = pl.ds(pl.multiple_of(i * tile, tile), tile)
        totals[:, at] = jnp.dot(
            features[:, pl.ds(first, width)],
            rows_all[pl.ds(first, width), at],
            preferred_element_type=jnp.float32,
        )

    take(other, 10)

    @pl.loop(0, width // tile)
    def _(i):
        at = pl.ds(pl.multiple_of(i * tile, tile), tile)
        more = jnp.dot(
            features[:, pl.ds(second, width)],
            rows_all[pl.ds(second, width), at],
            preferred_element_type=jnp.float32,
        )
        out[:, at] = (totals[:, at] + more).astype(out.dtype)

    weight_sent()

    def sent(view, slot, own=False):
        pltpu.make_async_copy(view, view, own_sem.at[slot] if own else send_sem.at[slot]).wait()

    final.wait_send()
    relay(in_spec_one, 4).wait_send()
    relay(in_spec_two, 6).wait_send()
    most = pl.ds(0, count - 1)
    for slot in (0, 1, 2, 9):
        sent(in_signal.at[most], slot)

    @pl.when(g != m)
    def _():
        for slot in (0, 1, 2, 9):
            sent(in_signal.at[0], slot, True)
        sent(in_skip.at[0], 7, True)
        sent(in_skip.at[1], 8, True)

    @pl.when(g == m)
    def _():
        for slot in (3, 5):
            sent(in_spec_one.at[:, most], slot)
            sent(in_spec_one.at[0, 0], slot, True)


def direct_shards(
    signal,
    gate_first,
    gate_second,
    spectrum_first,
    spectrum_second,
    skip_first,
    skip_second,
    out_weight,
):
    count = lax.axis_size("seq")
    span, width = signal.shape
    cols = width // count
    coarse = 2 * count
    anywhere = pl.BlockSpec(memory_space=pltpu.HBM)
    vmem = pl.BlockSpec(memory_space=pltpu.VMEM)
    bf16, f32 = jnp.bfloat16, jnp.float32
    return pl.pallas_call(
        functools.partial(block_kernel, count),
        out_shape=jax.ShapeDtypeStruct((span, width), bf16),
        in_specs=[anywhere] * 8 + [vmem],
        out_specs=vmem,
        scratch_shapes=[
            pltpu.VMEM((count, span, cols), bf16),
            pltpu.VMEM((count, span, cols), bf16),
            pltpu.VMEM((count, span, cols), bf16),
            pltpu.VMEM((2, count, 2, span, cols), bf16),
            pltpu.VMEM((2, count, 2, span, cols), bf16),
            pltpu.VMEM((2, count, cols), f32),
            pltpu.VMEM((coarse, 2, 2 * span, 2 * span), bf16),
            pltpu.VMEM((coarse, 2, 2 * span, 2 * span), bf16),
            pltpu.VMEM((4, span, span), f32),
            pltpu.VMEM((count + 1, 2 * span, 2 * cols), bf16),
            pltpu.VMEM((coarse, 2 * span, cols), f32),
            pltpu.VMEM((count, span, cols), bf16),
            pltpu.VMEM((count, span, cols), bf16),
            pltpu.VMEM((span, 2 * width), bf16),
            pltpu.VMEM((span, width), f32),
            pltpu.VMEM((2 * width, width), bf16),
            pltpu.SemaphoreType.DMA((11,)),
            pltpu.SemaphoreType.DMA((11,)),
            pltpu.SemaphoreType.DMA((11,)),
            pltpu.SemaphoreType.DMA((2, count // 2)),
            pltpu.SemaphoreType.DMA((count // 2,)),
            pltpu.SemaphoreType.DMA((count // 2,)),
            pltpu.SemaphoreType.DMA((count // 2,)),
            pltpu.SemaphoreType.DMA((count,)),
            pltpu.SemaphoreType.DMA((count,)),
            pltpu.SemaphoreType.DMA((1,)),
        ],
        compiler_params=pltpu.CompilerParams(
            collective_id=0, has_side_effects=True, vmem_limit_bytes=62 * 1024 * 1024
        ),
        cost_estimate=pl.CostEstimate(
            flops=16 * coarse * span * span * cols, bytes_accessed=1 << 26, transcendentals=0
        ),
    )(
        signal,
        gate_first,
        gate_second,
        spectrum_first,
        spectrum_second,
        skip_first.reshape(count, cols),
        skip_second.reshape(count, cols),
        out_weight,
        jnp.asarray(turn_tables(span, coarse)),
    )


def shards(*arrays):
    count = lax.axis_size("seq")
    span, width = arrays[0].shape
    pairs = lax.axis_size("grp") == 2 and lax.axis_size("mdl") == 2
    whole_tiles = width == count * LANES and span == LANES and count == 8
    if pairs and whole_tiles and arrays[3].shape[1] == 2:
        return direct_shards(*arrays)
    return plain_shards(*arrays)


def solution(mesh):
    placed = (
        P(("grp", "seq"), "mdl"),
        P(("grp", "seq"), "mdl"),
        P(("grp", "seq"), "mdl"),
        P(None, "seq", None, "mdl"),
        P(None, "seq", None, "mdl"),
        P("mdl"),
        P("mdl"),
        P("seq", "mdl"),
    )
    return jax.shard_map(
        shards, mesh=mesh, in_specs=placed, out_specs=P(("grp", "seq"), "mdl"), check_vma=False
    )
```

```python
import functools
import math

import jax
import jax.numpy as jnp
import numpy as np
from jax import lax
from jax.experimental import pallas as pl
from jax.experimental.pallas import tpu as pltpu
from jax.sharding import PartitionSpec as P

MESH = pl.DeviceIdType.MESH
LANES = 128


def angle_grid(first, second, modulus):
    product = first[:, None] * second[None, :] % modulus
    angles = product.astype(jnp.float32) * (2.0 * math.pi / modulus)
    return (jnp.cos(angles), jnp.sin(angles))


def mixing(form, left, right):
    return jnp.einsum(form, left, right, precision=lax.Precision.HIGHEST)


def complex_mix(form, real_table, imag_table, values_re, values_im):
    first_term = mixing(form, real_table, values_re + values_im)
    second_term = mixing(form, real_table + imag_table, values_im)
    third_term = mixing(form, imag_table - real_table, values_re)
    return (first_term - second_term, first_term + third_term)


def channel_filter(field, spectrum):
    coarse = spectrum.shape[1]
    span = spectrum.shape[2]
    count = coarse // 2
    cols = field.shape[1]
    length = coarse * span
    pencil = field.reshape(count, span, cols)
    coarse_ids = jnp.arange(coarse, dtype=jnp.int32)
    cos_a, sin_a = angle_grid(coarse_ids, jnp.arange(count, dtype=jnp.int32), coarse)
    part_re = mixing("ka,amc->kmc", cos_a, pencil)
    part_im = -mixing("ka,amc->kmc", sin_a, pencil)
    fine_ids = jnp.arange(span, dtype=jnp.int32)
    cos_t, sin_t = angle_grid(coarse_ids, fine_ids, length)
    cos_t = cos_t[:, :, None]
    sin_t = sin_t[:, :, None]
    turned_re = part_re * cos_t + part_im * sin_t
    turned_im = part_im * cos_t - part_re * sin_t
    cos_s, sin_s = angle_grid(fine_ids, fine_ids, span)
    full_re, full_im = complex_mix("qm,kmc->kqc", cos_s, -sin_s, turned_re, turned_im)
    filt_re = spectrum[0].astype(jnp.float32)
    filt_im = spectrum[1].astype(jnp.float32)
    prod_re = filt_re * full_re - filt_im * full_im
    prod_im = filt_re * full_im + filt_im * full_re
    inner_re, inner_im = complex_mix("mq,kqc->kmc", cos_s, sin_s, prod_re, prod_im)
    back_re = inner_re * cos_t - inner_im * sin_t
    back_im = inner_im * cos_t + inner_re * sin_t
    result = mixing("ka,kmc->amc", cos_a, back_re) - mixing("ka,kmc->amc", sin_a, back_im)
    return (result / length).reshape(count * span, cols)


def plain_shards(
    signal,
    gate_first,
    gate_second,
    spectrum_first,
    spectrum_second,
    skip_first,
    skip_second,
    out_weight,
):
    seq_index = lax.axis_index("seq")
    width = signal.shape[1]
    parts_seq = lax.axis_size("seq")
    cols = width // parts_seq
    col_sig, col_first, col_second = (
        lax.all_to_all(signal, "seq", split_axis=1, concat_axis=0, tiled=True),
        lax.all_to_all(gate_first, "seq", split_axis=1, concat_axis=0, tiled=True),
        lax.all_to_all(gate_second, "seq", split_axis=1, concat_axis=0, tiled=True),
    )
    spec_one, spec_two = (
        lax.all_to_all(spectrum_first, "seq", split_axis=3, concat_axis=1, tiled=True),
        lax.all_to_all(spectrum_second, "seq", split_axis=3, concat_axis=1, tiled=True),
    )
    skip_one = lax.dynamic_slice_in_dim(skip_first, seq_index * cols, cols, 0)
    skip_two = lax.dynamic_slice_in_dim(skip_second, seq_index * cols, cols, 0)
    values = col_sig.astype(jnp.float32)
    first_conv = channel_filter(values, spec_one) + skip_one * values
    first_out = (col_first.astype(jnp.float32) * first_conv).astype(jnp.bfloat16)
    first_vals = first_out.astype(jnp.float32)
    second_conv = channel_filter(first_vals, spec_two) + skip_two * first_vals
    mixed_cols = (col_second.astype(jnp.float32) * second_conv).astype(jnp.bfloat16)
    mixed = lax.all_to_all(mixed_cols, "seq", split_axis=0, concat_axis=1, tiled=True)
    features = lax.all_gather(mixed, "mdl", axis=1, tiled=True)
    total = jnp.dot(
        features,
        lax.all_gather(out_weight, "seq", axis=0, tiled=True),
        preferred_element_type=jnp.float32,
    )
    return total.astype(jnp.bfloat16)


def turn_tables(span, coarse):
    ids = np.arange(span)
    fine = 2.0 * math.pi * (ids[:, None] * ids[None, :] % span) / span
    step = 2.0 * math.pi * np.broadcast_to(ids[:, None], (span, span)) / (span * coarse)
    return np.stack(
        [np.cos(fine), np.sin(fine), np.cos(step), np.sin(step), np.cos(step).T, np.sin(step).T]
    ).astype(np.float32)


def weighted(terms):
    total = None
    for weight, value in terms:
        if abs(weight) < 1e-12:
            continue
        if abs(weight - 1.0) < 1e-12:
            term = value
        elif abs(weight + 1.0) < 1e-12:
            total = -value if total is None else total - value
            continue
        else:
            term = value * weight
        total = term if total is None else total + term
    return total


def coarse_forward(field, parts, rows):
    count, span, cols = field.shape
    half = count // 2

    @pl.loop(0, span // rows)
    def _(i):
        at = pl.multiple_of(i * rows, rows)
        f = [field[a, pl.ds(at, rows), :].astype(jnp.float32) for a in range(count)]
        plus = {a: f[a] + f[count - a] for a in range(1, half)}
        minus = {a: f[a] - f[count - a] for a in range(1, half)}
        for j in range(count + 1):
            for_cos, for_sin = (plus, minus) if j % 2 == 0 else (minus, plus)
            angle = [math.pi * a * j / count for a in range(count)]
            real = weighted(
                [(1.0, f[0]), (math.cos(angle[half]), f[half])]
                + [(math.cos(angle[a]), for_cos[a]) for a in range(1, half)]
            )
            imag = weighted(
                [(-math.sin(angle[half]), f[half])]
                + [(-math.sin(angle[a]), for_sin[a]) for a in range(1, half)]
            )
            if imag is None:
                imag = jnp.zeros_like(real)
            for top, value in ((at, real), (pl.multiple_of(span + at, rows), imag)):
                high = value.astype(jnp.bfloat16)
                parts[j, pl.ds(top, rows), :cols] = high
                parts[j, pl.ds(top, rows), cols:] = (value - high.astype(jnp.float32)).astype(
                    jnp.bfloat16
                )


def split_dot(table, j, both, cols):
    main = jnp.dot(table[j, 0], both, preferred_element_type=jnp.float32)
    rest = jnp.dot(table[j, 1], both[:, :cols], preferred_element_type=jnp.float32)
    return main[:, :cols] + (main[:, cols:] + rest)


def fine_stage(parts, spectrum, there, back_table, back, k, count, span):
    @pl.loop(0, count, unroll=4)
    def _(b):
        j = 2 * b + k
        source = jnp.where(j <= count, j, 2 * count - j)
        full = split_dot(there, j, parts[source], back.shape[2])
        full_re, full_im = full[:span], full[span:]
        filt_re = spectrum[k, b, 0].astype(jnp.float32)
        filt_im = spectrum[k, b, 1].astype(jnp.float32)
        prod_re = filt_re * full_re - filt_im * full_im
        prod_im = filt_re * full_im + filt_im * full_re
        prod = jnp.concatenate([prod_re, prod_im], axis=0)
        high = prod.astype(jnp.bfloat16)
        low = (prod - high.astype(jnp.float32)).astype(jnp.bfloat16)
        both = jnp.concatenate([high, low], axis=1)
        back[j] = split_dot(back_table, j, both, back.shape[2])


def coarse_back(back, field, gate, skip, result, rows):
    count, span, cols = field.shape
    half = count // 2
    direct = jnp.broadcast_to(skip, (rows, cols))

    @pl.loop(0, span // rows)
    def _(i):
        at = pl.multiple_of(i * rows, rows)
        low = pl.multiple_of(span + at, rows)

        def real(j):
            return back[j, pl.ds(at, rows), :]

        def imag(j):
            return back[j, pl.ds(low, rows), :]

        re = [real(0)] + [real(j) + real(2 * count - j) for j in range(1, count)] + [real(count)]
        im = [None] + [imag(j) - imag(2 * count - j) for j in range(1, count)] + [None]
        even_re = [re[j] + re[count - j] for j in range(half)]
        odd_re = [re[j] - re[count - j] for j in range(half)]
        even_im = [None] + [im[j] - im[count - j] for j in range(1, half)]
        odd_im = [None] + [im[j] + im[count - j] for j in range(1, half)]
        for a in range(count):
            use_re, use_im = (even_re, even_im) if a % 2 == 0 else (odd_re, odd_im)
            angle = [math.pi * a * j / count for j in range(half + 1)]
            total = weighted(
                [(math.cos(angle[j]), use_re[j]) for j in range(half)]
                + [(math.cos(angle[half]), re[half]), (-math.sin(angle[half]), im[half])]
                + [(-math.sin(angle[j]), use_im[j]) for j in range(1, half)]
            )
            values = field[a, pl.ds(at, rows), :].astype(jnp.float32)
            total = total + direct * values
            gated = gate[a, pl.ds(at, rows), :].astype(jnp.float32) * total
            result[a, pl.ds(at, rows), :] = gated.astype(jnp.bfloat16)


def build_tables(tab, there, back_table, turn, count, span):
    turn[0] = tab[0]
    turn[1] = tab[1]
    turn[2] = tab[0]
    turn[3] = tab[1]
    scale = 1.0 / (2 * count * span)

    @pl.loop(0, 2 * count)
    def _(j):
        flip = jnp.where(j > count, -1.0, 1.0).astype(jnp.float32)
        cos_a, sin_a, cos_b, sin_b = turn[0], turn[1], turn[2], turn[3]
        cos_s, sin_s = cos_b * scale, sin_b * scale
        entries = (
            (there, cos_a, sin_a * flip, -sin_a, cos_a * flip),
            (back_table, cos_s, -sin_s, sin_s, cos_s),
        )
        places = ((0, 0), (0, 1), (1, 0), (1, 1))
        for table, *blocks in entries:
            for (row, col), value in zip(places, blocks):
                at = (slice(row * span, row * span + span), slice(col * span, col * span + span))
                high = value.astype(jnp.bfloat16)
                table[(j, 0) + at] = high
                table[(j, 1) + at] = (value - high.astype(jnp.float32)).astype(jnp.bfloat16)
        turn[0] = cos_a * tab[4] - sin_a * tab[5]
        turn[1] = sin_a * tab[4] + cos_a * tab[5]
        turn[2] = cos_b * tab[2] - sin_b * tab[3]
        turn[3] = sin_b * tab[2] + cos_b * tab[3]


def block_kernel(
    count,
    signal,
    gate_one,
    gate_two,
    spec_one,
    spec_two,
    skip_one,
    skip_two,
    weight,
    tab,
    out,
    in_signal,
    in_gate_one,
    in_gate_two,
    in_spec_one,
    in_spec_two,
    in_skip,
    there,
    back_table,
    turn,
    parts,
    back,
    second_field,
    mixed,
    features,
    totals,
    rows_all,
    send_sem,
    own_sem,
    recv_sem,
    line_send,
    line_recv,
    side_send,
    side_recv,
    plane_send,
    plane_recv,
    own_copy,
    mix_recv,
    pass_send,
):
    g, s, m = lax.axis_index("grp"), lax.axis_index("seq"), lax.axis_index("mdl")
    span, cols = in_signal.shape[1], in_signal.shape[2]
    total = 4 * count
    me = (g * count + s) * 2 + m

    barrier = pltpu.get_barrier_semaphore()

    @pl.loop(1, total)
    def _(o):
        peer = lax.rem(me + o, total)
        pl.semaphore_signal(
            barrier,
            inc=1,
            device_id=(peer // (2 * count), lax.rem(peer // 2, count), lax.rem(peer, 2)),
            device_id_type=MESH,
        )

    pl.semaphore_wait(barrier, total - 1)

    def columns(block):
        return pl.ds(pl.multiple_of(block * cols, cols), cols)

    def remote(source, target, slot, own, where):
        return pltpu.make_async_remote_copy(
            src_ref=source,
            dst_ref=target,
            send_sem=own_sem.at[slot] if own else send_sem.at[slot],
            recv_sem=recv_sem.at[slot],
            device_id=where,
            device_id_type=MESH,
        )

    def local(source, target, slot):
        return pltpu.make_async_copy(source, target, recv_sem.at[slot])

    def swap(source, target, slot):
        @pl.when(g == m)
        def _():
            local(source, target, slot).start()

        @pl.when(g != m)
        def _():
            remote(source, target, slot, True, (m, s, g)).start()

    def send_rows(array, buffer, slot):
        @pl.loop(1, count)
        def _(o):
            c = lax.rem(s + o, count)
            remote(array.at[:, columns(c)], buffer.at[s], slot, False, (m, c, g)).start()

        swap(array.at[:, columns(s)], buffer.at[s], slot)

    def send_spectrum(array, buffer, slot):
        @pl.when(g == m)
        def _():
            @pl.loop(1, count)
            def _(o):
                c = lax.rem(s + o, count)
                for k in range(2):
                    remote(
                        array.at[:, k, :, columns(c)], buffer.at[k, s], slot, False, (g, c, k)
                    ).start()

            remote(
                array.at[:, 1 - m, :, columns(s)], buffer.at[1 - m, s], slot, True, (g, s, 1 - m)
            ).start()
            local(array.at[:, m, :, columns(s)], buffer.at[m, s], slot).start()

    def relay(buffer, slot):
        return remote(buffer.at[m], buffer.at[m], slot, False, (g, s, 1 - m))

    def take(view, slot):
        pltpu.make_async_copy(view, view, recv_sem.at[slot]).wait()

    levels = count // 2
    z, x = s // 2, lax.rem(s, 2)
    beside = s + 1 - 2 * x
    depth = weight.shape[0]
    piece = depth // 2

    def chunk(block, half):
        return rows_all.at[pl.ds(pl.multiple_of(block * depth + half * piece, piece), piece), :]

    def post(block, source, sems, where):
        return pltpu.make_async_remote_copy(
            src_ref=source,
            dst_ref=chunk(block, g),
            send_sem=sems[0],
            recv_sem=sems[1],
            device_id=where,
            device_id_type=MESH,
        )

    def along(block, source, way):
        level = block // 2
        step = 2 if way == 0 else -2
        return post(
            block, source, (line_send.at[way, level], line_recv.at[level]), (g, s + step, m)
        )

    def across(block, source):
        level = block // 2
        return post(block, source, (side_send.at[level], side_recv.at[level]), (g, beside, m))

    def over(block):
        return post(
            block, chunk(block, g), (plane_send.at[block], plane_recv.at[block]), (1 - g, s, m)
        )

    def landed(block, half, sem):
        view = chunk(block, half)
        pltpu.make_async_copy(view, view, sem).wait()

    own_rows = pltpu.make_async_copy(
        weight, rows_all.at[pl.ds(pl.multiple_of(s * depth, depth), depth), :], own_copy.at[0]
    )
    own_piece = weight.at[pl.ds(pl.multiple_of(g * piece, piece), piece), :]

    def weight_step(distance):
        if distance == 0:
            own_rows.start()

            @pl.when(z < levels - 1)
            def _():
                along(s, own_piece, 0).start()

            @pl.when(z > 0)
            def _():
                along(s, own_piece, 1).start()

            across(s, own_piece).start()
            return

        @pl.when(z >= distance)
        def _():
            block = s - 2 * distance
            landed(block, g, line_recv.at[z - distance])

            @pl.when(z < levels - 1)
            def _():
                along(block, chunk(block, g), 0).start()

            across(block, chunk(block, g)).start()
            over(block).start()

        @pl.when(z + distance < levels)
        def _():
            block = s + 2 * distance
            landed(block, g, line_recv.at[z + distance])

            @pl.when(z > 0)
            def _():
                along(block, chunk(block, g), 1).start()

            across(block, chunk(block, g)).start()
            over(block).start()

    def weight_side(distance):
        @pl.when(z >= distance)
        def _():
            block = beside - 2 * distance
            landed(block, g, side_recv.at[z - distance])
            over(block).start()

        if distance > 0:

            @pl.when(z + distance < levels)
            def _():
                block = beside + 2 * distance
                landed(block, g, side_recv.at[z + distance])
                over(block).start()

    def weight_end():
        own_rows.wait()

        @pl.loop(1, count)
        def _(o):
            block = lax.rem(s + o, count)
            landed(block, 1 - g, plane_recv.at[block])

    def weight_sent():
        for distance in range(levels):

            @pl.when((z >= distance) & (z < levels - 1))
            def _():
                along(s - 2 * distance, chunk(0, g), 0).wait_send()

            @pl.when((z + distance < levels) & (z > 0))
            def _():
                along(s + 2 * distance, chunk(0, g), 1).wait_send()

        @pl.loop(0, levels)
        def _(level):
            across(2 * level + x, chunk(0, g)).wait_send()

        @pl.loop(1, count)
        def _(o):
            over(lax.rem(s + o, count)).wait_send()

    send_rows(signal, in_signal, 0)
    weight_step(0)
    send_spectrum(spec_one, in_spec_one, 3)
    send_rows(gate_one, in_gate_one, 1)
    swap(skip_one, in_skip.at[0], 7)
    swap(skip_two, in_skip.at[1], 8)

    build_tables(tab, there, back_table, turn, count, span)

    weight_step(1)
    weight_side(0)
    take(in_signal, 0)
    coarse_forward(in_signal, parts, 16)
    weight_step(2)
    weight_side(1)
    send_rows(gate_two, in_gate_two, 2)
    send_spectrum(spec_two, in_spec_two, 5)
    take(in_spec_one.at[m], 3)
    relay(in_spec_one, 4).start()
    fine_stage(parts, in_spec_one, there, back_table, back, m, count, span)
    take(in_spec_one.at[1 - m], 4)
    fine_stage(parts, in_spec_one, there, back_table, back, 1 - m, count, span)
    take(in_gate_one, 1)
    take(in_skip.at[0], 7)
    take(in_skip.at[1], 8)
    weight_step(3)
    weight_side(2)
    coarse_back(back, in_signal, in_gate_one, in_skip[0, pl.ds(s, 1), :], second_field, 16)
    coarse_forward(second_field, parts, 16)
    take(in_spec_two.at[m], 5)
    relay(in_spec_two, 6).start()
    weight_side(3)
    fine_stage(parts, in_spec_two, there, back_table, back, m, count, span)
    take(in_spec_two.at[1 - m], 6)
    fine_stage(parts, in_spec_two, there, back_table, back, 1 - m, count, span)
    take(in_gate_two, 2)
    coarse_back(back, second_field, in_gate_two, in_skip[1, pl.ds(s, 1), :], mixed, 16)

    width = count * cols
    mine = columns(g * count + s)

    def deliver(block, own=False):
        return pltpu.make_async_remote_copy(
            src_ref=mixed.at[block],
            dst_ref=features.at[:, mine],
            send_sem=own_sem.at[9] if own else send_sem.at[9],
            recv_sem=mix_recv.at[s],
            device_id=(m, block, g),
            device_id_type=MESH,
        )

    def pass_on(block):
        view = features.at[:, columns(m * count + block)]
        return pltpu.make_async_remote_copy(
            src_ref=view,
            dst_ref=view,
            send_sem=pass_send.at[block],
            recv_sem=recv_sem.at[10],
            device_id=(g, s, 1 - m),
            device_id_type=MESH,
        )

    @pl.when(g == m)
    def _():
        pltpu.make_async_copy(mixed.at[s], features.at[:, mine], mix_recv.at[s]).start()

    @pl.when(g != m)
    def _():
        deliver(s, True).start()

    @pl.loop(1, count)
    def _(o):
        deliver(lax.rem(s + o, count)).start()

    weight_end()
    first = pl.multiple_of(m * width, width)
    second = pl.multiple_of((1 - m) * width, width)
    other = features.at[:, pl.ds(second, width)]

    @pl.loop(0, count)
    def _(o):
        block = lax.rem(s + count - o, count)
        view = features.at[:, columns(m * count + block)]
        pltpu.make_async_copy(view, view, mix_recv.at[block]).wait()
        pass_on(block).start()

    tile = 2 * cols

    @pl.loop(0, width // tile)
    def _(i):
        at = pl.ds(pl.multiple_of(i * tile, tile), tile)
        totals[:, at] = jnp.dot(
            features[:, pl.ds(first, width)],
            rows_all[pl.ds(first, width), at],
            preferred_element_type=jnp.float32,
        )

    take(other, 10)

    @pl.loop(0, width // tile)
    def _(i):
        at = pl.ds(pl.multiple_of(i * tile, tile), tile)
        more = jnp.dot(
            features[:, pl.ds(second, width)],
            rows_all[pl.ds(second, width), at],
            preferred_element_type=jnp.float32,
        )
        out[:, at] = (totals[:, at] + more).astype(out.dtype)

    weight_sent()

    def sent(view, slot, own=False):
        pltpu.make_async_copy(view, view, own_sem.at[slot] if own else send_sem.at[slot]).wait()


    @pl.loop(0, count)
    def _(block):
        pass_on(block).wait_send()

    relay(in_spec_one, 4).wait_send()
    relay(in_spec_two, 6).wait_send()
    most = pl.ds(0, count - 1)
    for slot in (0, 1, 2, 9):
        sent(in_signal.at[most], slot)

    @pl.when(g != m)
    def _():
        for slot in (0, 1, 2, 9):
            sent(in_signal.at[0], slot, True)
        sent(in_skip.at[0], 7, True)
        sent(in_skip.at[1], 8, True)

    @pl.when(g == m)
    def _():
        for slot in (3, 5):
            sent(in_spec_one.at[:, most], slot)
            sent(in_spec_one.at[0, 0], slot, True)


def direct_shards(
    signal,
    gate_first,
    gate_second,
    spectrum_first,
    spectrum_second,
    skip_first,
    skip_second,
    out_weight,
):
    count = lax.axis_size("seq")
    span, width = signal.shape
    cols = width // count
    coarse = 2 * count
    anywhere = pl.BlockSpec(memory_space=pltpu.HBM)
    vmem = pl.BlockSpec(memory_space=pltpu.VMEM)
    bf16, f32 = jnp.bfloat16, jnp.float32
    return pl.pallas_call(
        functools.partial(block_kernel, count),
        out_shape=jax.ShapeDtypeStruct((span, width), bf16),
        in_specs=[anywhere] * 8 + [vmem],
        out_specs=vmem,
        scratch_shapes=[
            pltpu.VMEM((count, span, cols), bf16),
            pltpu.VMEM((count, span, cols), bf16),
            pltpu.VMEM((count, span, cols), bf16),
            pltpu.VMEM((2, count, 2, span, cols), bf16),
            pltpu.VMEM((2, count, 2, span, cols), bf16),
            pltpu.VMEM((2, count, cols), f32),
            pltpu.VMEM((coarse, 2, 2 * span, 2 * span), bf16),
            pltpu.VMEM((coarse, 2, 2 * span, 2 * span), bf16),
            pltpu.VMEM((4, span, span), f32),
            pltpu.VMEM((count + 1, 2 * span, 2 * cols), bf16),
            pltpu.VMEM((coarse, 2 * span, cols), f32),
            pltpu.VMEM((count, span, cols), bf16),
            pltpu.VMEM((count, span, cols), bf16),
            pltpu.VMEM((span, 2 * width), bf16),
            pltpu.VMEM((span, width), f32),
            pltpu.VMEM((2 * width, width), bf16),
            pltpu.SemaphoreType.DMA((11,)),
            pltpu.SemaphoreType.DMA((11,)),
            pltpu.SemaphoreType.DMA((11,)),
            pltpu.SemaphoreType.DMA((2, count // 2)),
            pltpu.SemaphoreType.DMA((count // 2,)),
            pltpu.SemaphoreType.DMA((count // 2,)),
            pltpu.SemaphoreType.DMA((count // 2,)),
            pltpu.SemaphoreType.DMA((count,)),
            pltpu.SemaphoreType.DMA((count,)),
            pltpu.SemaphoreType.DMA((1,)),
            pltpu.SemaphoreType.DMA((count,)),
            pltpu.SemaphoreType.DMA((count,)),
        ],
        compiler_params=pltpu.CompilerParams(
            collective_id=0, has_side_effects=True, vmem_limit_bytes=62 * 1024 * 1024
        ),
        cost_estimate=pl.CostEstimate(
            flops=16 * coarse * span * span * cols, bytes_accessed=1 << 26, transcendentals=0
        ),
    )(
        signal,
        gate_first,
        gate_second,
        spectrum_first,
        spectrum_second,
        skip_first.reshape(count, cols),
        skip_second.reshape(count, cols),
        out_weight,
        jnp.asarray(turn_tables(span, coarse)),
    )


def shards(*arrays):
    count = lax.axis_size("seq")
    span, width = arrays[0].shape
    pairs = lax.axis_size("grp") == 2 and lax.axis_size("mdl") == 2
    whole_tiles = width == count * LANES and span == LANES and count == 8
    if pairs and whole_tiles and arrays[3].shape[1] == 2:
        return direct_shards(*arrays)
    return plain_shards(*arrays)


def solution(mesh):
    placed = (
        P(("grp", "seq"), "mdl"),
        P(("grp", "seq"), "mdl"),
        P(("grp", "seq"), "mdl"),
        P(None, "seq", None, "mdl"),
        P(None, "seq", None, "mdl"),
        P("mdl"),
        P("mdl"),
        P("seq", "mdl"),
    )
    return jax.shard_map(
        shards, mesh=mesh, in_specs=placed, out_specs=P(("grp", "seq"), "mdl"), check_vma=False
    )
```
